32 devices in a mesh: pb: 8 (over z, core), ka: 4 (over y, x).
Axes of the slice: x: 2, y: 2, z: 4, core: 2. Of those that a mesh axis runs over, the one named last changes fastest.
Arguments:
- activations: bfloat16 [4, 1024, 768], P(None, ('pb', 'ka')), may hold values from -6 to 6
- attn_gain: float32 [768], replicated, may hold values from 0.1 to 1.9
- w_qkv: bfloat16 [768, 2304], replicated, may hold values from -0.21875 to 0.21875
- w_gate: bfloat16 [768, 768], replicated, may hold values from -0.21875 to 0.21875
- w_out: bfloat16 [768, 768], replicated, may hold values from -0.21875 to 0.21875
- pair_bias: bfloat16 [16, 1024, 1024], P(None, 'pb', 'ka'), may hold values from -240 to 240
- chain_ids: int32 [1024], replicated, may hold values from 0 to 5, as said below
- binder_flag: int32 [1024], replicated, may hold values from 0 to 1, as said below
- trans_gain: float32 [768], replicated, may hold values from 0.1 to 1.9
- w_up: bfloat16 [768, 3072], replicated, may hold values from -0.21875 to 0.21875
- w_down: bfloat16 [1536, 768], replicated, may hold values from -0.15625 to 0.15625
Outputs:
- updated: bfloat16 [4, 1024, 768], P(None, ('pb', 'ka'))
The draws below stay inside these ranges and needn't reach their ends.
Inputs may be any that keep to these rules, and one draw needn't show every extreme that they name: `chain_ids`: chain ids never fall along the tokens; every chain has at least one token. `binder_flag`: all tokens of one chain carry the same flag.
All inputs are finite; a program needn't handle non-finite values.
Results may differ from the reference program's by a relative error of at most 0.0056.
Values may be sent and summed in bfloat16 or wider, within the bound.
No kernel may reach another device: no remote copies, remote signals or barrier semaphores. Data moves between devices by JAX's collectives and lax.ppermute only.
A program may use at most 128 MiB of HBM per device.

```python
import math
import jax
import jax.numpy as jnp
from jax import lax

D = 768
HEADS = 16
FF = 1536
SAMPLES = 4
CHAINS = 6
TOKENS = 1024
N_PB = 8
N_KA = 4


peak_count = 6


def chain_layout(key):
    cut_key = jax.random.fold_in(key, 11)
    pick_key = jax.random.fold_in(key, 12)
    cut_order = jax.random.permutation(cut_key, TOKENS - 1)[:CHAINS - 1] + 1
    cut_points = jnp.sort(cut_order.astype(jnp.int32))
    positions = jnp.arange(TOKENS, dtype=jnp.int32)
    chain_table = jnp.sum((positions[:, None] >= cut_points[None, :]).astype(jnp.int32), axis=1).astype(jnp.int32)
    chain_picks = jax.random.randint(pick_key, (CHAINS,), 0, 4)
    binder_chain = ((chain_picks == 0) | (jnp.arange(CHAINS, dtype=jnp.int32) == CHAINS - 1)).astype(jnp.int32)
    return (chain_table, binder_chain[chain_table])


def draw_chain_ids(key, part):
    return chain_layout(key)[0]


def draw_binder_flag(key, part):
    return chain_layout(key)[1]


def add_peaks(key, base_bias):
    column_key = jax.random.fold_in(key, 23)
    height_key = jax.random.fold_in(key, 24)
    columns = jax.random.randint(column_key, (HEADS, TOKENS, peak_count), 0, TOKENS)
    heights = jax.random.uniform(height_key, (HEADS, TOKENS, peak_count), jnp.float32, 6.0, 11.0)
    head_index = jnp.broadcast_to(jnp.arange(HEADS, dtype=jnp.int32)[:, None, None], columns.shape)
    row_index = jnp.broadcast_to(jnp.arange(TOKENS, dtype=jnp.int32)[None, :, None], columns.shape)
    return base_bias.at[head_index, row_index, columns].add(heights)


def draw_pair_bias(key, part):
    base_key = jax.random.fold_in(key, 21)
    base_bias = jnp.clip(jax.random.normal(base_key, (HEADS, TOKENS, TOKENS), jnp.float32), -6.0, 6.0)
    return add_peaks(key, base_bias).astype(jnp.bfloat16)


def block_scale(own_key, dims, shards, low, high):
    def one(axis_at, parts):
        steps = jax.random.uniform(jax.random.fold_in(jax.random.fold_in(own_key, 6), axis_at), (parts,), jnp.float32, low / len(shards), high / len(shards))
        return jnp.repeat(jnp.exp(steps), dims[axis_at] // parts).reshape((-1,) + (1,) * (len(dims) - axis_at - 1))

    factor_of = one(*shards[0])
    for cut in shards[1:]:
        factor_of = factor_of * one(*cut)
    return factor_of


def noise(rng, dims, width, limit, cuts=(), kind=jnp.bfloat16):
    array = jax.random.normal(rng, dims, jnp.float32) * width
    if len(cuts) > 0:
        array = block_scale(rng, dims, cuts, -0.22, 0.18) * array
    return jnp.clip(array, min=-limit, max=limit).astype(kind)


def setup_inputs(seed: int = 0) -> dict:
    key_of = jax.random.split(jax.random.key(seed), 12)
    activations = noise(key_of[0], (SAMPLES, TOKENS, D), 1.0, 6.0, ((1, 32),))
    attn_gain = jnp.clip(1.0 + 0.18 * jax.random.normal(key_of[1], (D,), jnp.float32), 0.1, 1.9)
    w_qkv = noise(key_of[2], (D, 3 * D), D ** -0.5, 0.21875)
    w_gate = noise(key_of[3], (D, D), D ** -0.5, 0.21875)
    w_out = noise(key_of[4], (D, D), D ** -0.5, 0.21875)
    pair_bias = draw_pair_bias(jax.random.fold_in(key_of[11], 71), 0)
    chain_ids = draw_chain_ids(jax.random.fold_in(key_of[11], 71), 0)
    binder_flag = draw_binder_flag(jax.random.fold_in(key_of[11], 71), 0)
    trans_gain = jnp.clip(1.0 + 0.18 * jax.random.normal(key_of[8], (D,), jnp.float32), 0.1, 1.9)
    w_up = noise(key_of[9], (D, 2 * FF), D ** -0.5, 0.21875)
    w_down = noise(key_of[10], (FF, D), FF ** -0.5, 0.15625)
    return dict(activations=activations, attn_gain=attn_gain, w_qkv=w_qkv, w_gate=w_gate, w_out=w_out, pair_bias=pair_bias, chain_ids=chain_ids, binder_flag=binder_flag, trans_gain=trans_gain, w_up=w_up, w_down=w_down)


epsilon = 1e-05
masked_score = -1000000000.0

def layer_norm(values, scales):
    centred = values - lax.optimization_barrier(jnp.mean(values, axis=-1, keepdims=True))
    spread = lax.optimization_barrier(jnp.mean(centred * centred, axis=-1, keepdims=True))
    return centred * lax.rsqrt(spread + epsilon) * scales

def widened(values):
    return lax.optimization_barrier(values).astype(jnp.float32)

def block_stats(query_rows, key_block, value_block, bias_tile, allowed):
    head_count = bias_tile.shape[0]
    query_heads = widened(query_rows).reshape(query_rows.shape[0], head_count, -1)
    key_heads = widened(key_block).reshape(key_block.shape[0], head_count, -1)
    value_heads = widened(value_block).reshape(value_block.shape[0], head_count, -1)
    head_size = query_heads.shape[-1]
    scores = jnp.einsum('qhd,khd->hqk', query_heads, key_heads) / math.sqrt(head_size)
    scores = scores + bias_tile.astype(jnp.float32)
    best_score = lax.optimization_barrier(jnp.max(jnp.where(allowed[None], scores, masked_score), axis=-1))
    weights = jnp.where(allowed[None], jnp.exp(scores - best_score[..., None]), 0.0)
    row_sum = lax.optimization_barrier(jnp.sum(weights, axis=-1))
    rounded = widened(weights.astype(jnp.bfloat16))
    block_out = jnp.einsum('hqk,khd->qhd', rounded, value_heads).reshape(query_rows.shape[0], -1)
    return (best_score.T, row_sum.T, block_out)

def reference(activations, attn_gain, w_qkv, w_gate, w_out, pair_bias, chain_ids, binder_flag, trans_gain, w_up, w_down):
    samples, token_count, model_width = activations.shape
    head_count = pair_bias.shape[0]
    normed = layer_norm(activations.astype(jnp.float32), attn_gain).astype(jnp.bfloat16)
    flat_normed = normed.reshape(-1, model_width)
    projected = jnp.dot(flat_normed, w_qkv, preferred_element_type=jnp.float32)
    projected = projected.reshape(samples, token_count, 3 * model_width)
    queries = projected[..., :model_width].astype(jnp.bfloat16)
    key_rows = projected[..., model_width:2 * model_width].astype(jnp.bfloat16)
    value_rows = projected[..., 2 * model_width:].astype(jnp.bfloat16)
    gate_pre = jnp.dot(flat_normed, w_gate, preferred_element_type=jnp.float32)
    gate_pre = gate_pre.reshape(samples, token_count, model_width)
    query_count = token_count // N_PB
    key_count = token_count // N_KA
    stats_per_sample = jax.vmap(block_stats, in_axes=(0, 0, 0, None, None))

    def query_block(block_index):
        start = (block_index * query_count).astype(jnp.int32)
        query_rows = lax.dynamic_slice_in_dim(queries, start, query_count, 1)
        row_chain = lax.dynamic_slice_in_dim(chain_ids, start, query_count, 0)
        row_binder = lax.dynamic_slice_in_dim(binder_flag, start, query_count, 0)
        block_tops, block_sums, block_outs = ([], [], [])
        for key_index in range(N_KA):
            lowest = key_index * key_count
            col_chain = chain_ids[lowest:lowest + key_count]
            col_binder = binder_flag[lowest:lowest + key_count]
            allowed = (row_binder[:, None] > 0) | (col_binder[None, :] > 0) | (row_chain[:, None] == col_chain[None, :])
            bias_tile = lax.dynamic_slice(pair_bias, (jnp.zeros((), jnp.int32), start, jnp.full((), lowest, jnp.int32)), (head_count, query_count, key_count))
            best_score, row_sum, block_out = stats_per_sample(query_rows, key_rows[:, lowest:lowest + key_count], value_rows[:, lowest:lowest + key_count], bias_tile, allowed)
            block_tops.append(best_score)
            block_sums.append(row_sum)
            block_outs.append(block_out)
        block_tops = jnp.stack(block_tops)
        block_sums = jnp.stack(block_sums)
        block_outs = jnp.stack(block_outs)
        overall = lax.optimization_barrier(jnp.max(block_tops, axis=0))
        factors = jnp.exp(block_tops - overall)
        row_sum = lax.optimization_barrier(jnp.sum(factors * block_sums, axis=0))
        shaped = block_outs.reshape(block_outs.shape[:-1] + (head_count, -1))
        summed = lax.optimization_barrier(jnp.sum(factors[..., None] * shaped, axis=0))
        return (summed / row_sum[..., None]).reshape(samples, query_count, model_width)
    attention = lax.map(query_block, jnp.arange(N_PB, dtype=jnp.int32))
    attention = jnp.moveaxis(attention, 0, 1).reshape(samples, token_count, model_width)
    gated = (jax.nn.sigmoid(gate_pre) * attention).astype(jnp.bfloat16)
    mixed = activations.astype(jnp.float32) + jnp.dot(gated.reshape(-1, model_width), w_out, preferred_element_type=jnp.float32).reshape(samples, token_count, model_width)
    trans_normed = layer_norm(mixed, trans_gain).astype(jnp.bfloat16)
    both_parts = jnp.dot(trans_normed.reshape(-1, model_width), w_up, preferred_element_type=jnp.float32)
    hidden_width = w_down.shape[0]
    hidden = (jax.nn.silu(both_parts[:, :hidden_width]) * both_parts[:, hidden_width:]).astype(jnp.bfloat16)
    updated = mixed + jnp.dot(hidden, w_down, preferred_element_type=jnp.float32).reshape(samples, token_count, model_width)
    return updated.astype(jnp.bfloat16)
```

```python
import functools
import math

import jax
import jax.numpy as jnp
from jax import lax
from jax.experimental import pallas as pl
from jax.experimental.pallas import tpu as pltpu
from jax.sharding import PartitionSpec as P

epsilon = 1e-05
masked_score = -1500000000.0
log2e = math.log2(math.e)
lanes = 128
window = 256
f32 = jnp.float32
bf16 = jnp.bfloat16
nt = (((1,), (1,)), ((), ()))
tn = (((0,), (0,)), ((), ()))


def whole():
    return pl.BlockSpec(memory_space=pltpu.VMEM)


def cost(flops, moved):
    return pl.CostEstimate(flops=int(flops), bytes_accessed=int(moved), transcendentals=0)


def partner(i, step, n):
    return i ^ step if n & (n - 1) == 0 else (step - i) % n


def layer_norm(values, scales):
    centred = values - jnp.mean(values, axis=-1, keepdims=True)
    spread = jnp.mean(centred * centred, axis=-1, keepdims=True)
    return centred * lax.rsqrt(spread + epsilon) * scales


def norm_kernel(x_ref, gain_ref, out_ref):
    out_ref[...] = layer_norm(x_ref[...].astype(f32), gain_ref[...]).astype(bf16)


def gate_kernel(x_ref, w_ref, out_ref):
    gate = jnp.dot(x_ref[...], w_ref[...], preferred_element_type=f32)
    out_ref[...] = jax.nn.sigmoid(gate).T


def pair_start(first, size, width):
    span = min(window, width)
    return min(first * size // lanes * lanes, width - span)


def query_kernel(heads, scale, *refs):
    *piece_refs, w_ref, out_ref = refs
    samples, rows, width = piece_refs[0].shape
    size = width // heads
    count = len(piece_refs) * rows
    span = out_ref.shape[-1]
    column = lax.broadcasted_iota(jnp.int32, (samples * rows, span), 1)
    for at, piece in enumerate(piece_refs):
        flat = piece[...].reshape(samples * rows, width)
        made = jnp.dot(flat, w_ref[...], preferred_element_type=f32) * scale
        for head in range(heads):
            start = pair_start(head // 2 * 2, size, width)
            kept = (column >= head * size - start) & (column < (head + 1) * size - start)
            picked = jnp.where(kept, made[:, start : start + span], 0.0).astype(bf16)
            spot = head % 2 * count + at * rows
            out_ref[:, head // 2, spot : spot + rows, :] = picked.reshape(samples, rows, span)


def bias_kernel(n, rows, place_ref, row_ref, col_ref, bias_ref, out_ref, turned, flipped):
    query_count, key_count = bias_ref.shape[1:]
    group, core, ka = place_ref[0], place_ref[1], place_ref[2]
    cores = key_count // query_count
    row_code, col_code = row_ref[...], col_ref[...]
    allowed = (row_code < 0) | (col_code < 0) | (row_code == col_code)
    turned[...] = jnp.where(allowed, bias_ref[0].astype(f32) * log2e, masked_score)
    ordered = [
        turned[pl.ds(pl.multiple_of(partner(ka, step, n) * rows, rows), rows), :]
        for step in range(n)
    ]
    flipped[...] = jnp.concatenate(ordered, axis=0).T
    for shift in range(cores):
        for step in range(n):
            source = lax.rem(core + cores - shift, cores) * query_count
            source = pl.multiple_of(source + partner(group, step, n) * rows, rows)
            spot = (shift * n + step) * rows
            out_ref[0, spot : spot + rows, :] = flipped[pl.ds(source, rows), :]


def attention_kernel(heads, *refs):
    (*piece_refs, q_ref, wk_ref, wv_ref, bias_ref, out_ref, x_buf, k_buf, v_buf) = refs
    rows, width = piece_refs[0].shape[1:]
    size = width // heads
    query_count = q_ref.shape[2] // 2
    sample = pl.program_id(0)
    for at, piece in enumerate(piece_refs):
        x_buf[at * rows : (at + 1) * rows, :] = piece[0]
    k_buf[...] = jnp.dot(x_buf[...], wk_ref[...], preferred_element_type=f32).astype(bf16)
    v_buf[...] = lax.dot_general(wv_ref[...], x_buf[...], nt, preferred_element_type=f32).astype(
        bf16
    )
    spot = sample * rows
    tile = pl.multiple_of(spot // lanes * lanes, lanes)
    within = spot % lanes
    lane = lax.broadcasted_iota(jnp.int32, (size, lanes), 1)
    mine = (lane >= within) & (lane < within + rows)
    lane_one = lax.broadcasted_iota(jnp.int32, (heads, lanes), 1)
    mine_one = (lane_one >= within) & (lane_one < within + rows)

    def put(values, first, count, mask):
        for at in range(query_count // rows):
            source = at * rows // lanes * lanes
            turn = lax.rem(within + lanes - at * rows % lanes, lanes)
            moved = pltpu.roll(values[:, source : source + lanes], turn, 1)
            spot = (at, slice(first, first + count), pl.ds(tile, lanes))
            out_ref[spot] = jnp.where(mask, moved, out_ref[spot].astype(f32)).astype(bf16)

    tops, sums = [], []
    span = q_ref.shape[-1]
    for first in range(0, heads, 2):
        start = pair_start(first, size, width)
        scores = lax.dot_general(
            k_buf[:, start : start + span],
            q_ref[0, first // 2],
            nt,
            preferred_element_type=f32,
        )
        for at in range(2):
            head = first + at
            score = scores[:, at * query_count : (at + 1) * query_count] + bias_ref[head]
            top = jnp.max(score, axis=0, keepdims=True)
            weight = jnp.exp2(score - top)
            total = jnp.sum(weight, axis=0, keepdims=True)
            made = jnp.dot(
                v_buf[head * size : (head + 1) * size, :],
                weight.astype(bf16),
                preferred_element_type=f32,
            )
            put(made * (1.0 / total), head * size, size, mine)
            tops.append(top)
            sums.append(total)
    level = jnp.concatenate(tops, axis=0) + jnp.log2(jnp.concatenate(sums, axis=0))
    for part in range(3):
        rounded = level.astype(bf16).astype(f32)
        put(rounded, width + part * heads, heads, mine_one)
        level = level - rounded


def finish_kernel(heads, *refs):
    *part_refs, gate_ref, act_ref, wo_ref, gain_ref, up_ref, down_ref, out_ref = refs
    width = act_ref.shape[-1]
    size = width // heads
    levels = []
    for part in part_refs:
        tail = part[width : width + 3 * heads, :].astype(f32)
        levels.append(tail[:heads] + (tail[heads : 2 * heads] + tail[2 * heads :]))
    best = functools.reduce(jnp.maximum, levels)
    shares = [jnp.exp2(level - best) for level in levels]
    inverse = 1.0 / functools.reduce(jnp.add, shares)
    shares = [share * inverse for share in shares]
    blocks = []
    for head in range(heads):
        where = slice(head * size, (head + 1) * size)
        merged = functools.reduce(
            jnp.add,
            [
                share[head : head + 1] * part[where, :].astype(f32)
                for share, part in zip(shares, part_refs)
            ],
        )
        blocks.append(merged * gate_ref[where, :])
    gated = jnp.concatenate(blocks, axis=0).T.astype(bf16)
    mixed = act_ref[...].astype(f32) + jnp.dot(gated, wo_ref[...], preferred_element_type=f32)
    normed = layer_norm(mixed, gain_ref[...]).astype(bf16)
    both = jnp.dot(normed, up_ref[...], preferred_element_type=f32)
    hidden = both.shape[1] // 2
    left = both[:, :hidden]
    made = (left / (1.0 + jnp.exp(-left)) * both[:, hidden:]).astype(bf16)
    out_ref[...] = (mixed + jnp.dot(made, down_ref[...], preferred_element_type=f32)).astype(bf16)


def body(
    activations,
    attn_gain,
    w_qkv,
    w_gate,
    w_out,
    pair_bias,
    chain_ids,
    binder_flag,
    trans_gain,
    w_up,
    w_down,
):
    samples, rows, width = activations.shape
    heads, query_count, key_count = pair_bias.shape
    n = lax.axis_size("ka")
    cores = lax.axis_size("pb") // n
    flat_rows = samples * rows
    pb, ka = lax.axis_index("pb"), lax.axis_index("ka")
    group, core = pb // cores, pb % cores

    normed = pl.pallas_call(
        norm_kernel,
        out_shape=jax.ShapeDtypeStruct((flat_rows, width), bf16),
        in_specs=[whole(), whole()],
        out_specs=whole(),
        name="norm",
        cost_estimate=cost(10 * flat_rows * width, 4 * flat_rows * width),
    )(activations.reshape(flat_rows, width), attn_gain.reshape(1, width))
    own = normed.reshape(samples, rows, width)

    def spread(value, step):
        pairs = []
        for g in range(n):
            for c in range(cores):
                for j in range(n):
                    target = (partner(j, step, n) * cores + c) * n + g
                    pairs.append(((g * cores + c) * n + j, target))
        return lax.ppermute(value, ("pb", "ka"), pairs)

    def swap(value, step):
        pairs = [
            (g * cores + c, g * cores + (c + step) % cores)
            for g in range(n)
            for c in range(cores)
        ]
        return lax.ppermute(value, "pb", pairs)

    def exchange(value, step):
        pairs = [(j, partner(j, step, n)) for j in range(n)]
        if all(a == b for a, b in pairs):
            return value
        return lax.ppermute(value, "ka", pairs)

    key_pieces = [spread(own, step) for step in range(n)]
    query_pieces = [exchange(own, step) for step in range(n)]
    for step in range(1, cores):
        key_pieces = key_pieces + [swap(piece, step) for piece in key_pieces[:n]]

    gate = pl.pallas_call(
        gate_kernel,
        out_shape=jax.ShapeDtypeStruct((width, flat_rows), f32),
        in_specs=[whole(), whole()],
        out_specs=whole(),
        name="gate",
        cost_estimate=cost(2 * flat_rows * width * width, 2 * width * width),
    )(normed, w_gate)

    code = jnp.where(binder_flag > 0, -1, chain_ids).astype(jnp.int32)
    row_code = lax.dynamic_slice_in_dim(code, pb * query_count, query_count, 0)
    col_code = lax.dynamic_slice_in_dim(code, ka * key_count, key_count, 0)
    place = jnp.stack([group, core, ka]).astype(jnp.int32)
    bias = pl.pallas_call(
        functools.partial(bias_kernel, n, rows),
        grid_spec=pltpu.PrefetchScalarGridSpec(
            num_scalar_prefetch=1,
            grid=(heads,),
            in_specs=[
                pl.BlockSpec((query_count, 1), lambda h, place: (0, 0)),
                pl.BlockSpec((1, key_count), lambda h, place: (0, 0)),
                pl.BlockSpec((1, query_count, key_count), lambda h, place: (h, 0, 0)),
            ],
            out_specs=pl.BlockSpec((1, key_count, query_count), lambda h, place: (h, 0, 0)),
            scratch_shapes=[
                pltpu.VMEM((query_count, key_count), f32),
                pltpu.VMEM((key_count, query_count), f32),
            ],
        ),
        out_shape=jax.ShapeDtypeStruct((heads, key_count, query_count), f32),
        name="bias",
        cost_estimate=cost(
            8 * heads * key_count * query_count, 6 * heads * key_count * query_count
        ),
    )(place, row_code.reshape(-1, 1), col_code.reshape(1, -1), pair_bias)

    size = width // heads
    span = min(window, width)
    masked = (samples, heads // 2, 2 * query_count, span)
    queries = pl.pallas_call(
        functools.partial(query_kernel, heads, log2e / math.sqrt(size)),
        grid=(1,),
        out_shape=jax.ShapeDtypeStruct(masked, bf16),
        in_specs=[pl.BlockSpec((samples, rows, width), lambda i: (0, 0, 0))] * n
        + [pl.BlockSpec((width, width), lambda i: (0, 0))],
        out_specs=pl.BlockSpec(masked, lambda i: (0, 0, 0, 0)),
        name="queries",
        cost_estimate=cost(
            2 * n * flat_rows * width * width, 2 * width * width + 2 * math.prod(masked)
        ),
    )(*query_pieces, w_qkv)

    value_weights = w_qkv[:, 2 * width :].T
    depth = width + 3 * heads
    once = dict(pipeline_mode=pl.Buffered(1))
    message = (n, depth, flat_rows)
    parts = pl.pallas_call(
        functools.partial(attention_kernel, heads),
        grid=(samples,),
        out_shape=jax.ShapeDtypeStruct(message, bf16),
        in_specs=[pl.BlockSpec((1, rows, width), lambda s: (s, 0, 0))] * (cores * n)
        + [
            pl.BlockSpec((1,) + masked[1:], lambda s: (s, 0, 0, 0)),
            pl.BlockSpec((width, width), lambda s: (0, 1), **once),
            pl.BlockSpec((width, width), lambda s: (0, 0), **once),
            pl.BlockSpec((heads, key_count, query_count), lambda s: (0, 0, 0), **once),
        ],
        out_specs=pl.BlockSpec(message, lambda s: (0, 0, 0)),
        scratch_shapes=[
            pltpu.VMEM((key_count, width), bf16),
            pltpu.VMEM((key_count, width), bf16),
            pltpu.VMEM((width, key_count), bf16),
        ],
        name="attention",
        cost_estimate=cost(
            4 * samples * key_count * width * width, 4 * heads * key_count * query_count
        ),
    )(*key_pieces, queries, w_qkv, value_weights, bias)
    parts = [exchange(parts[step], step) for step in range(n)]

    updated = pl.pallas_call(
        functools.partial(finish_kernel, heads),
        out_shape=jax.ShapeDtypeStruct((flat_rows, width), bf16),
        in_specs=[whole()] * (n + 6),
        out_specs=whole(),
        name="finish",
        cost_estimate=cost(
            2 * flat_rows * width * width * 7, 14 * width * width
        ),
    )(
        *parts,
        gate,
        activations.reshape(flat_rows, width),
        w_out,
        trans_gain.reshape(1, width),
        w_up,
        w_down,
    )
    return updated.reshape(samples, rows, width)


def solution(mesh):
    placed = (
        P(None, ("pb", "ka"), None),
        P(),
        P(),
        P(),
        P(),
        P(None, "pb", "ka"),
        P(),
        P(),
        P(),
        P(),
        P(),
    )
    return jax.shard_map(
        body, mesh=mesh, in_specs=placed, out_specs=P(None, ("pb", "ka"), None), check_vma=False
    )
```

```python
import functools
import math

import jax
import jax.numpy as jnp
from jax import lax
from jax.experimental import pallas as pl
from jax.experimental.pallas import tpu as pltpu
from jax.sharding import PartitionSpec as P

epsilon = 1e-05
masked_score = -1500000000.0
log2e = math.log2(math.e)
lanes = 128
window = 256
f32 = jnp.float32
bf16 = jnp.bfloat16
nt = (((1,), (1,)), ((), ()))
tn = (((0,), (0,)), ((), ()))


def whole():
    return pl.BlockSpec(memory_space=pltpu.VMEM)


def cost(flops, moved):
    return pl.CostEstimate(flops=int(flops), bytes_accessed=int(moved), transcendentals=0)


def partner(i, step, n):
    return i ^ step if n & (n - 1) == 0 else (step - i) % n


def layer_norm(values, scales):
    centred = values - jnp.mean(values, axis=-1, keepdims=True)
    spread = jnp.mean(centred * centred, axis=-1, keepdims=True)
    return centred * lax.rsqrt(spread + epsilon) * scales


def norm_kernel(x_ref, gain_ref, out_ref):
    out_ref[...] = layer_norm(x_ref[...].astype(f32), gain_ref[...].reshape(1, -1)).astype(bf16)


def gate_kernel(x_ref, w_ref, out_ref):
    gate = jnp.dot(x_ref[...], w_ref[...], preferred_element_type=f32)
    out_ref[...] = jax.nn.sigmoid(gate).T


def pair_start(first, size, width):
    span = min(window, width)
    return min(first * size // lanes * lanes, width - span)


def query_kernel(heads, scale, *refs):
    *piece_refs, w_ref, out_ref = refs
    samples, rows, width = piece_refs[0].shape
    size = width // heads
    count = len(piece_refs) * rows
    span = out_ref.shape[-1]
    column = lax.broadcasted_iota(jnp.int32, (samples * rows, span), 1)
    for at, piece in enumerate(piece_refs):
        flat = piece[...].reshape(samples * rows, width)
        made = jnp.dot(flat, w_ref[...], preferred_element_type=f32) * scale
        for head in range(heads):
            start = pair_start(head // 2 * 2, size, width)
            kept = (column >= head * size - start) & (column < (head + 1) * size - start)
            picked = jnp.where(kept, made[:, start : start + span], 0.0).astype(bf16)
            spot = head % 2 * count + at * rows
            out_ref[:, head // 2, spot : spot + rows, :] = picked.reshape(samples, rows, span)


def bias_kernel(n, rows, chain_ref, binder_ref, bias_ref, out_ref, turned, flipped):
    query_count, key_count = bias_ref.shape[1:]
    cores = key_count // query_count
    pb, ka = lax.axis_index("pb"), lax.axis_index("ka")
    group, core = lax.div(pb, cores), lax.rem(pb, cores)

    def codes(first, count):
        spot = pl.ds(pl.multiple_of(first, count), count)
        made = jnp.where(binder_ref[spot] > 0, -1, chain_ref[spot]).astype(f32)
        return made.reshape(1, count)

    col_code = codes(ka * key_count, key_count)
    row_code = codes(pb * query_count, query_count)
    row_code = jnp.broadcast_to(row_code, (lanes, query_count)).T[:, :1]
    allowed = (row_code < 0) | (col_code < 0) | (row_code == col_code)
    turned[...] = jnp.where(allowed, bias_ref[0].astype(f32) * log2e, masked_score)
    ordered = [
        turned[pl.ds(pl.multiple_of(partner(ka, step, n) * rows, rows), rows), :]
        for step in range(n)
    ]
    flipped[...] = jnp.concatenate(ordered, axis=0).T
    for shift in range(cores):
        for step in range(n):
            source = lax.rem(core + cores - shift, cores) * query_count
            source = pl.multiple_of(source + partner(group, step, n) * rows, rows)
            spot = (shift * n + step) * rows
            out_ref[0, spot : spot + rows, :] = flipped[pl.ds(source, rows), :]


def attention_kernel(heads, pieces, *refs):
    inputs, (x_buf, k_buf, v_buf) = refs[: pieces + 4], refs[-3:]
    *piece_refs, q_ref, wk_ref, wv_ref, bias_ref = inputs
    out_refs = refs[pieces + 4 : -3]
    rows, width = piece_refs[0].shape[1:]
    size = width // heads
    query_count = q_ref.shape[2] // 2
    sample = pl.program_id(0)
    for at, piece in enumerate(piece_refs):
        x_buf[at * rows : (at + 1) * rows, :] = piece[0]
    k_buf[...] = jnp.dot(x_buf[...], wk_ref[...], preferred_element_type=f32).astype(bf16)
    v_buf[...] = lax.dot_general(wv_ref[...], x_buf[...], nt, preferred_element_type=f32).astype(
        bf16
    )
    spot = sample * rows
    tile = pl.multiple_of(spot // lanes * lanes, lanes)
    within = spot % lanes
    lane = lax.broadcasted_iota(jnp.int32, (size, lanes), 1)
    mine = (lane >= within) & (lane < within + rows)
    lane_one = lax.broadcasted_iota(jnp.int32, (heads, lanes), 1)
    mine_one = (lane_one >= within) & (lane_one < within + rows)

    def put(values, first, count, mask):
        for at in range(query_count // rows):
            source = at * rows // lanes * lanes
            turn = lax.rem(within + lanes - at * rows % lanes, lanes)
            moved = pltpu.roll(values[:, source : source + lanes], turn, 1)
            out_ref, spot = out_refs[at], (slice(first, first + count), pl.ds(tile, lanes))
            out_ref[spot] = jnp.where(mask, moved, out_ref[spot].astype(f32)).astype(bf16)

    tops, sums = [], []
    span = q_ref.shape[-1]
    for first in range(0, heads, 2):
        start = pair_start(first, size, width)
        scores = lax.dot_general(
            k_buf[:, start : start + span],
            q_ref[0, first // 2],
            nt,
            preferred_element_type=f32,
        )
        for at in range(2):
            head = first + at
            score = scores[:, at * query_count : (at + 1) * query_count] + bias_ref[head]
            top = jnp.max(score, axis=0, keepdims=True)
            weight = jnp.exp2(score - top)
            total = jnp.sum(weight, axis=0, keepdims=True)
            made = jnp.dot(
                v_buf[head * size : (head + 1) * size, :],
                weight.astype(bf16),
                preferred_element_type=f32,
            )
            put(made * (1.0 / total), head * size, size, mine)
            tops.append(top)
            sums.append(total)
    level = jnp.concatenate(tops, axis=0) + jnp.log2(jnp.concatenate(sums, axis=0))
    for part in range(3):
        rounded = level.astype(bf16).astype(f32)
        put(rounded, width + part * heads, heads, mine_one)
        level = level - rounded


def finish_kernel(heads, *refs):
    *part_refs, gate_ref, act_ref, wo_ref, gain_ref, up_ref, down_ref, out_ref = refs
    width = act_ref.shape[-1]
    size = width // heads
    levels = []
    for part in part_refs:
        tail = part[width : width + 3 * heads, :].astype(f32)
        levels.append(tail[:heads] + (tail[heads : 2 * heads] + tail[2 * heads :]))
    best = functools.reduce(jnp.maximum, levels)
    shares = [jnp.exp2(level - best) for level in levels]
    inverse = 1.0 / functools.reduce(jnp.add, shares)
    shares = [share * inverse for share in shares]
    blocks = []
    for head in range(heads):
        where = slice(head * size, (head + 1) * size)
        merged = functools.reduce(
            jnp.add,
            [
                share[head : head + 1] * part[where, :].astype(f32)
                for share, part in zip(shares, part_refs)
            ],
        )
        blocks.append(merged * gate_ref[where, :])
    gated = jnp.concatenate(blocks, axis=0).T.astype(bf16)
    mixed = act_ref[...].astype(f32) + jnp.dot(gated, wo_ref[...], preferred_element_type=f32)
    normed = layer_norm(mixed, gain_ref[...].reshape(1, -1)).astype(bf16)
    both = jnp.dot(normed, up_ref[...], preferred_element_type=f32)
    hidden = both.shape[1] // 2
    left = both[:, :hidden]
    made = (left / (1.0 + jnp.exp(-left)) * both[:, hidden:]).astype(bf16)
    out_ref[...] = (mixed + jnp.dot(made, down_ref[...], preferred_element_type=f32)).astype(bf16)


def body(
    activations,
    attn_gain,
    w_qkv,
    w_gate,
    w_out,
    pair_bias,
    chain_ids,
    binder_flag,
    trans_gain,
    w_up,
    w_down,
):
    samples, rows, width = activations.shape
    heads, query_count, key_count = pair_bias.shape
    n = lax.axis_size("ka")
    cores = lax.axis_size("pb") // n
    flat_rows = samples * rows

    normed = pl.pallas_call(
        norm_kernel,
        out_shape=jax.ShapeDtypeStruct((flat_rows, width), bf16),
        in_specs=[whole(), whole()],
        out_specs=whole(),
        name="norm",
        cost_estimate=cost(10 * flat_rows * width, 4 * flat_rows * width),
    )(activations.reshape(flat_rows, width), attn_gain)
    own = normed.reshape(samples, rows, width)

    def spread(value, step):
        pairs = []
        for g in range(n):
            for c in range(cores):
                for j in range(n):
                    target = (partner(j, step, n) * cores + c) * n + g
                    pairs.append(((g * cores + c) * n + j, target))
        return lax.ppermute(value, ("pb", "ka"), pairs)

    def swap(value, step):
        pairs = [
            (g * cores + c, g * cores + (c + step) % cores)
            for g in range(n)
            for c in range(cores)
        ]
        return lax.ppermute(value, "pb", pairs)

    def exchange(value, step):
        pairs = [(j, partner(j, step, n)) for j in range(n)]
        if all(a == b for a, b in pairs):
            return value
        return lax.ppermute(value, "ka", pairs)

    key_pieces = [spread(own, step) for step in range(n)]
    query_pieces = [exchange(own, step) for step in range(n)]

    gate = pl.pallas_call(
        gate_kernel,
        out_shape=jax.ShapeDtypeStruct((width, flat_rows), f32),
        in_specs=[whole(), whole()],
        out_specs=whole(),
        name="gate",
        cost_estimate=cost(2 * flat_rows * width * width, 2 * width * width),
    )(normed, w_gate)

    bias = pl.pallas_call(
        functools.partial(bias_kernel, n, rows),
        grid=(heads,),
        in_specs=[
            pl.BlockSpec(chain_ids.shape, lambda h: (0,)),
            pl.BlockSpec(chain_ids.shape, lambda h: (0,)),
            pl.BlockSpec((1, query_count, key_count), lambda h: (h, 0, 0)),
        ],
        out_specs=pl.BlockSpec((1, key_count, query_count), lambda h: (h, 0, 0)),
        scratch_shapes=[
            pltpu.VMEM((query_count, key_count), f32),
            pltpu.VMEM((key_count, query_count), f32),
        ],
        out_shape=jax.ShapeDtypeStruct((heads, key_count, query_count), f32),
        name="bias",
        cost_estimate=cost(
            8 * heads * key_count * query_count, 6 * heads * key_count * query_count
        ),
    )(chain_ids, binder_flag, pair_bias)
    value_weights = w_qkv[:, 2 * width :].T
    bias, gate, value_weights = lax.optimization_barrier((bias, gate, value_weights))
    key_pieces = [lax.optimization_barrier((piece, bias, gate))[0] for piece in key_pieces]
    for step in range(1, cores):
        key_pieces = key_pieces + [swap(piece, step) for piece in key_pieces[:n]]

    size = width // heads
    span = min(window, width)
    masked = (samples, heads // 2, 2 * query_count, span)
    queries = pl.pallas_call(
        functools.partial(query_kernel, heads, log2e / math.sqrt(size)),
        grid=(1,),
        out_shape=jax.ShapeDtypeStruct(masked, bf16),
        in_specs=[pl.BlockSpec((samples, rows, width), lambda i: (0, 0, 0))] * n
        + [pl.BlockSpec((width, width), lambda i: (0, 0))],
        out_specs=pl.BlockSpec(masked, lambda i: (0, 0, 0, 0)),
        name="queries",
        cost_estimate=cost(
            2 * n * flat_rows * width * width, 2 * width * width + 2 * math.prod(masked)
        ),
    )(*query_pieces, w_qkv)

    depth = width + 3 * heads
    once = dict(pipeline_mode=pl.Buffered(1))
    message = (depth, flat_rows)
    parts = pl.pallas_call(
        functools.partial(attention_kernel, heads, cores * n),
        grid=(samples,),
        out_shape=[jax.ShapeDtypeStruct(message, bf16)] * n,
        in_specs=[pl.BlockSpec((1, rows, width), lambda s: (s, 0, 0))] * (cores * n)
        + [
            pl.BlockSpec((1,) + masked[1:], lambda s: (s, 0, 0, 0)),
            pl.BlockSpec((width, width), lambda s: (0, 1), **once),
            pl.BlockSpec((width, width), lambda s: (0, 0), **once),
            pl.BlockSpec((heads, key_count, query_count), lambda s: (0, 0, 0), **once),
        ],
        out_specs=[pl.BlockSpec(message, lambda s: (0, 0))] * n,
        scratch_shapes=[
            pltpu.VMEM((key_count, width), bf16),
            pltpu.VMEM((key_count, width), bf16),
            pltpu.VMEM((width, key_count), bf16),
        ],
        name="attention",
        cost_estimate=cost(
            4 * samples * key_count * width * width, 4 * heads * key_count * query_count
        ),
    )(*key_pieces, queries, w_qkv, value_weights, bias)
    parts = [exchange(parts[step], step) for step in range(n)]

    updated = pl.pallas_call(
        functools.partial(finish_kernel, heads),
        out_shape=jax.ShapeDtypeStruct((flat_rows, width), bf16),
        in_specs=[whole()] * (n + 6),
        out_specs=whole(),
        name="finish",
        cost_estimate=cost(
            2 * flat_rows * width * width * 7, 14 * width * width
        ),
    )(
        *parts,
        gate,
        activations.reshape(flat_rows, width),
        w_out,
        trans_gain,
        w_up,
        w_down,
    )
    return updated.reshape(samples, rows, width)


def solution(mesh):
    placed = (
        P(None, ("pb", "ka"), None),
        P(),
        P(),
        P(),
        P(),
        P(None, "pb", "ka"),
        P(),
        P(),
        P(),
        P(),
        P(),
    )
    return jax.shard_map(
        body, mesh=mesh, in_specs=placed, out_specs=P(None, ("pb", "ka"), None), check_vma=False
    )
```

```python
import functools
import math

import jax
import jax.numpy as jnp
from jax import lax
from jax.experimental import pallas as pl
from jax.experimental.pallas import tpu as pltpu
from jax.sharding import PartitionSpec as P

epsilon = 1e-05
masked_score = -1500000000.0
log2e = math.log2(math.e)
lanes = 128
window = 256
grant = 14 << 20
f32 = jnp.float32
bf16 = jnp.bfloat16
nt = (((1,), (1,)), ((), ()))
tn = (((0,), (0,)), ((), ()))


def whole():
    return pl.BlockSpec(memory_space=pltpu.VMEM)


def held(value):
    return pltpu.with_memory_space_constraint(value, pltpu.VMEM)


def call(kernel, name, outs, operands, flops, moved, scratch=(), grid=(), near=True, last=False):
    made = pl.pallas_call(
        kernel,
        grid=grid,
        out_shape=[jax.ShapeDtypeStruct(*out) if last else pltpu.VMEM(*out) for out in outs],
        in_specs=[whole()] * len(operands),
        out_specs=[whole()] * len(outs),
        scratch_shapes=list(scratch),
        compiler_params=pltpu.CompilerParams(vmem_limit_bytes=grant),
        name=name,
        cost_estimate=cost(flops, moved),
    )(*[held(operand) if near else operand for operand in operands])
    return made if len(outs) > 1 else made[0]


def cost(flops, moved):
    return pl.CostEstimate(flops=int(flops), bytes_accessed=int(moved), transcendentals=0)


def partner(i, step, n):
    return i ^ step if n & (n - 1) == 0 else (step - i) % n


def layer_norm(values, scales):
    centred = values - jnp.mean(values, axis=-1, keepdims=True)
    spread = jnp.mean(centred * centred, axis=-1, keepdims=True)
    return centred * lax.rsqrt(spread + epsilon) * scales


def norm_kernel(x_ref, gain_ref, out_ref):
    out_ref[...] = layer_norm(x_ref[...].astype(f32), gain_ref[...].reshape(1, -1)).astype(bf16)


def gate_kernel(x_ref, w_ref, out_ref):
    gate = jnp.dot(x_ref[...], w_ref[...], preferred_element_type=f32)
    out_ref[...] = jax.nn.sigmoid(gate).T


def pair_start(first, size, width):
    span = min(window, width)
    return min(first * size // lanes * lanes, width - span)


def query_kernel(heads, scale, *refs):
    *piece_refs, w_ref, out_ref = refs
    samples, rows, width = piece_refs[0].shape
    size = width // heads
    count = len(piece_refs) * rows
    span = out_ref.shape[-1]
    column = lax.broadcasted_iota(jnp.int32, (samples * rows, span), 1)
    for at, piece in enumerate(piece_refs):
        flat = piece[...].reshape(samples * rows, width)
        made = jnp.dot(flat, w_ref[:, :width], preferred_element_type=f32) * scale
        for head in range(heads):
            start = pair_start(head // 2 * 2, size, width)
            kept = (column >= head * size - start) & (column < (head + 1) * size - start)
            picked = jnp.where(kept, made[:, start : start + span], 0.0).astype(bf16)
            spot = head % 2 * count + at * rows
            out_ref[:, head // 2, spot : spot + rows, :] = picked.reshape(samples, rows, span)


def bias_kernel(n, rows, chain_ref, binder_ref, bias_ref, out_ref, turned, flipped):
    query_count, key_count = bias_ref.shape[1:]
    cores = key_count // query_count
    pb, ka = lax.axis_index("pb"), lax.axis_index("ka")
    group, core = lax.div(pb, cores), lax.rem(pb, cores)

    def codes(first, count):
        spot = pl.ds(pl.multiple_of(first, count), count)
        made = jnp.where(binder_ref[spot] > 0, -1, chain_ref[spot]).astype(f32)
        return made.reshape(1, count)

    col_code = codes(ka * key_count, key_count)
    row_code = codes(pb * query_count, query_count)
    row_code = jnp.broadcast_to(row_code, (lanes, query_count)).T[:, :1]
    allowed = (row_code < 0) | (col_code < 0) | (row_code == col_code)
    query_from = [pl.multiple_of(partner(ka, step, n) * rows, rows) for step in range(n)]
    key_from = [
        pl.multiple_of(
            lax.rem(core + cores - shift, cores) * query_count + partner(group, step, n) * rows,
            rows,
        )
        for shift in range(cores)
        for step in range(n)
    ]

    @pl.loop(0, bias_ref.shape[0])
    def _(head):
        biased = bias_ref[head].astype(f32) * log2e
        turned[...] = jnp.where(allowed, biased, masked_score)
        ordered = [turned[pl.ds(source, rows), :] for source in query_from]
        flipped[...] = jnp.concatenate(ordered, axis=0).T
        for at, source in enumerate(key_from):
            out_ref[head, at * rows : (at + 1) * rows, :] = flipped[pl.ds(source, rows), :]


def attention_kernel(heads, pieces, *refs):
    inputs, (x_buf, k_buf, v_buf) = refs[: pieces + 4], refs[-3:]
    *piece_refs, q_ref, w_ref, wv_ref, bias_ref = inputs
    out_refs = refs[pieces + 4 : -3]
    rows, width = piece_refs[0].shape[1:]
    size = width // heads
    query_count = q_ref.shape[2] // 2
    sample = pl.program_id(0)
    for at, piece in enumerate(piece_refs):
        x_buf[at * rows : (at + 1) * rows, :] = piece[sample]
    wk = w_ref[:, width : 2 * width]
    k_buf[...] = jnp.dot(x_buf[...], wk, preferred_element_type=f32).astype(bf16)
    v_buf[...] = lax.dot_general(wv_ref[...], x_buf[...], nt, preferred_element_type=f32).astype(
        bf16
    )
    spot = sample * rows
    tile = pl.multiple_of(spot // lanes * lanes, lanes)
    within = spot % lanes
    lane = lax.broadcasted_iota(jnp.int32, (size, lanes), 1)
    mine = (lane >= within) & (lane < within + rows)
    lane_one = lax.broadcasted_iota(jnp.int32, (heads, lanes), 1)
    mine_one = (lane_one >= within) & (lane_one < within + rows)

    def put(values, first, count, mask):
        for at in range(query_count // rows):
            source = at * rows // lanes * lanes
            turn = lax.rem(within + lanes - at * rows % lanes, lanes)
            moved = pltpu.roll(values[:, source : source + lanes], turn, 1)
            out_ref, spot = out_refs[at], (slice(first, first + count), pl.ds(tile, lanes))
            out_ref[spot] = jnp.where(mask, moved, out_ref[spot].astype(f32)).astype(bf16)

    tops, sums = [], []
    span = q_ref.shape[-1]
    for first in range(0, heads, 2):
        start = pair_start(first, size, width)
        scores = lax.dot_general(
            k_buf[:, start : start + span],
            q_ref[sample, first // 2],
            nt,
            preferred_element_type=f32,
        )
        for at in range(2):
            head = first + at
            score = scores[:, at * query_count : (at + 1) * query_count] + bias_ref[head]
            top = jnp.max(score, axis=0, keepdims=True)
            weight = jnp.exp2(score - top)
            total = jnp.sum(weight, axis=0, keepdims=True)
            made = jnp.dot(
                v_buf[head * size : (head + 1) * size, :],
                weight.astype(bf16),
                preferred_element_type=f32,
            )
            put(made * (1.0 / total), head * size, size, mine)
            tops.append(top)
            sums.append(total)
    level = jnp.concatenate(tops, axis=0) + jnp.log2(jnp.concatenate(sums, axis=0))
    for part in range(3):
        rounded = level.astype(bf16).astype(f32)
        put(rounded, width + part * heads, heads, mine_one)
        level = level - rounded


def finish_kernel(heads, *refs):
    *part_refs, gate_ref, act_ref, wo_ref, gain_ref, up_ref, down_ref, out_ref = refs
    width = act_ref.shape[-1]
    size = width // heads
    levels = []
    for part in part_refs:
        tail = part[width : width + 3 * heads, :].astype(f32)
        levels.append(tail[:heads] + (tail[heads : 2 * heads] + tail[2 * heads :]))
    best = functools.reduce(jnp.maximum, levels)
    shares = [jnp.exp2(level - best) for level in levels]
    inverse = 1.0 / functools.reduce(jnp.add, shares)
    shares = [share * inverse for share in shares]
    blocks = []
    for head in range(heads):
        where = slice(head * size, (head + 1) * size)
        merged = functools.reduce(
            jnp.add,
            [
                share[head : head + 1] * part[where, :].astype(f32)
                for share, part in zip(shares, part_refs)
            ],
        )
        blocks.append(merged * gate_ref[where, :])
    gated = jnp.concatenate(blocks, axis=0).T.astype(bf16)
    mixed = act_ref[...].astype(f32) + jnp.dot(gated, wo_ref[...], preferred_element_type=f32)
    normed = layer_norm(mixed, gain_ref[...].reshape(1, -1)).astype(bf16)
    both = jnp.dot(normed, up_ref[...], preferred_element_type=f32)
    hidden = both.shape[1] // 2
    left = both[:, :hidden]
    made = (left / (1.0 + jnp.exp(-left)) * both[:, hidden:]).astype(bf16)
    out_ref[...] = (mixed + jnp.dot(made, down_ref[...], preferred_element_type=f32)).astype(bf16)


def body(
    activations,
    attn_gain,
    w_qkv,
    w_gate,
    w_out,
    pair_bias,
    chain_ids,
    binder_flag,
    trans_gain,
    w_up,
    w_down,
):
    samples, rows, width = activations.shape
    heads, query_count, key_count = pair_bias.shape
    n = lax.axis_size("ka")
    cores = lax.axis_size("pb") // n
    flat_rows = samples * rows

    act_rows = activations.reshape(flat_rows, width)
    normed = call(
        norm_kernel,
        "norm",
        [((flat_rows, width), bf16)],
        [act_rows, attn_gain],
        10 * flat_rows * width,
        4 * flat_rows * width,
        near=False,
    )
    own = normed.reshape(samples, rows, width)

    def spread(value, step):
        pairs = []
        for g in range(n):
            for c in range(cores):
                for j in range(n):
                    target = (partner(j, step, n) * cores + c) * n + g
                    pairs.append(((g * cores + c) * n + j, target))
        return lax.ppermute(value, ("pb", "ka"), pairs)

    def swap(value, step):
        pairs = [
            (g * cores + c, g * cores + (c + step) % cores)
            for g in range(n)
            for c in range(cores)
        ]
        return lax.ppermute(value, "pb", pairs)

    def exchange(value, step):
        pairs = [(j, partner(j, step, n)) for j in range(n)]
        if all(a == b for a, b in pairs):
            return value
        return lax.ppermute(value, "ka", pairs)

    key_pieces = [spread(own, step) for step in range(n)]
    query_pieces = [exchange(own, step) for step in range(n)]

    gate = call(
        gate_kernel,
        "gate",
        [((width, flat_rows), f32)],
        [normed, w_gate],
        2 * flat_rows * width * width,
        2 * width * width,
    )
    bias = call(
        functools.partial(bias_kernel, n, rows),
        "bias",
        [((heads, key_count, query_count), f32)],
        [chain_ids, binder_flag, pair_bias],
        8 * heads * key_count * query_count,
        6 * heads * key_count * query_count,
        [
            pltpu.VMEM((query_count, key_count), f32),
            pltpu.VMEM((key_count, query_count), f32),
        ],
    )
    value_weights = w_qkv[:, 2 * width :].T
    bias, gate, value_weights = lax.optimization_barrier((bias, gate, value_weights))
    key_pieces = [lax.optimization_barrier((piece, bias, gate))[0] for piece in key_pieces]
    for step in range(1, cores):
        key_pieces = key_pieces + [swap(piece, step) for piece in key_pieces[:n]]

    size = width // heads
    span = min(window, width)
    masked = (samples, heads // 2, 2 * query_count, span)
    queries = call(
        functools.partial(query_kernel, heads, log2e / math.sqrt(size)),
        "queries",
        [(masked, bf16)],
        query_pieces + [w_qkv],
        2 * n * flat_rows * width * width,
        2 * width * width + 2 * math.prod(masked),
    )
    depth = width + 3 * heads
    parts = call(
        functools.partial(attention_kernel, heads, cores * n),
        "attention",
        [((depth, flat_rows), bf16)] * n,
        key_pieces + [queries, w_qkv, value_weights, bias],
        4 * samples * key_count * width * width,
        4 * heads * key_count * query_count,
        [
            pltpu.VMEM((key_count, width), bf16),
            pltpu.VMEM((key_count, width), bf16),
            pltpu.VMEM((width, key_count), bf16),
        ],
        (samples,),
    )
    parts = [exchange(parts[step], step) for step in range(n)]
    updated = call(
        functools.partial(finish_kernel, heads),
        "finish",
        [((flat_rows, width), bf16)],
        parts + [gate, act_rows, w_out, trans_gain, w_up, w_down],
        14 * flat_rows * width * width,
        14 * width * width,
        last=True,
    )
    return updated.reshape(samples, rows, width)


def solution(mesh):
    placed = (
        P(None, ("pb", "ka"), None),
        P(),
        P(),
        P(),
        P(),
        P(None, "pb", "ka"),
        P(),
        P(),
        P(),
        P(),
        P(),
    )
    return jax.shard_map(
        body, mesh=mesh, in_specs=placed, out_specs=P(None, ("pb", "ka"), None), check_vma=False
    )
```
